32 devices in a mesh: dev: 32 (over z, y, x, core).
Axes of the slice: x: 2, y: 2, z: 4, core: 2. Of those that a mesh axis runs over, the one named last changes fastest.
Arguments:
- grain_boxes: float32 [64, 64, 4096], P('dev'), may hold values from 0 to 1
- box_anchors: int32 [64, 3], P('dev'), may hold values from 0 to 31, as said below
- migrations: int32 [32, 2], P('dev'), may hold values from 0 to 1, as said below
Outputs:
- new_boxes: float32 [64, 64, 4096], P('dev')
The draws below stay inside these ranges and needn't reach their ends.
Inputs may be any that keep to these rules, and one draw needn't show every extreme that they name: `box_anchors`: box b belongs to device d = b // 2; its first coordinate is d - 1, d or d + 1 modulo 32; the other two coordinates are 0 to 3. `migrations`: the two entries of a row differ, so each device hands exactly one box to each neighbour and receives one from each.
All inputs are finite; a program needn't handle non-finite values.
Results may differ from the reference program's by a relative error of at most 0.0003.
Values sent between devices are 32-bit elements; how exact they have to be, the bound alone decides.
A program may use at most 128 MiB of HBM per device.

```python
import jax
import jax.numpy as jnp
from jax import lax

BOX = 64
BOX_DEV = 2
SUBSTEPS = 4
HALF = 32
TILE_YZ = 128
NX = 1024
BOXES = 64
N_DEV = 32


def draw_box_anchors(key, part):
    folded_key = jax.random.fold_in(key, 11)
    subkeys = jax.random.split(folded_key, 4)
    devices = BOXES // BOX_DEV
    offsets = jax.random.randint(subkeys[0], (BOXES,), -1, 2)
    first_box = jax.random.randint(subkeys[1], (), 0, BOX_DEV)
    final_box = (devices - 1) * BOX_DEV + jax.random.randint(subkeys[2], (), 0, BOX_DEV)
    box_index = jnp.arange(BOXES, dtype=jnp.int32)
    offsets = jnp.where(box_index == first_box, -1, offsets)
    offsets = jnp.where(box_index == final_box, 1, offsets)
    tile_first = (box_index // BOX_DEV + offsets) % devices
    lateral = jax.random.randint(subkeys[3], (BOXES, 2), 0, 4)
    return jnp.concatenate([tile_first[:, None], lateral], axis=1).astype(jnp.int32)


def draw_migrations(key, part):
    folded_key = jax.random.fold_in(key, 23)
    subkeys = jax.random.split(folded_key, 4)
    devices = BOXES // BOX_DEV
    right_slot = jax.random.randint(subkeys[0], (devices,), 0, BOX_DEV)
    row_index = jnp.arange(devices, dtype=jnp.int32)
    high_row = jax.random.randint(subkeys[1], (), 0, devices)
    low_row = (high_row + jax.random.randint(subkeys[2], (), 1, devices)) % devices
    right_slot = jnp.where(row_index == high_row, BOX_DEV - 1, right_slot)
    right_slot = jnp.where(row_index == low_row, 0, right_slot)
    left_slot = (right_slot + jax.random.randint(subkeys[3], (devices,), 1, BOX_DEV)) % BOX_DEV
    return jnp.stack([right_slot, left_slot], axis=1).astype(jnp.int32)


def shard_levels(rng, extent, pieces, least, largest):
    def one(axis_at, shards_of):
        heights = jax.random.uniform(jax.random.fold_in(jax.random.fold_in(rng, 6), axis_at), (shards_of,), jnp.float32, least / len(pieces), largest / len(pieces))
        return jnp.repeat(jnp.exp(heights), extent[axis_at] // shards_of).reshape((-1,) + (1,) * (len(extent) - axis_at - 1))

    gain = one(*pieces[0])
    for cut in pieces[1:]:
        gain = gain * one(*cut)
    return gain


def setup_inputs(seed: int = 0) -> dict:
    streams_of = jax.random.split(jax.random.key(seed), 4)
    grain_boxes = jnp.clip(1.0 * jax.random.uniform(streams_of[0], (BOXES, BOX, BOX * BOX), jnp.float32) ** shard_levels(streams_of[0], (BOXES, BOX, BOX * BOX), ((0, 32),), -0.2, 0.2), 0.0, 1.0)
    box_anchors = draw_box_anchors(jax.random.fold_in(streams_of[3], 71), 0)
    migrations = draw_migrations(jax.random.fold_in(streams_of[3], 71), 0)
    return dict(grain_boxes=grain_boxes, box_anchors=box_anchors, migrations=migrations)


growth_rate = 1.0
quartic_rate = 1.0
coupling = 1.5
gradient_energy = 2.0
time_step = 0.02


def laplacian(order_field):
    padded = jnp.pad(order_field, 1)
    beside = padded[2:, 1:-1, 1:-1] + padded[:-2, 1:-1, 1:-1]
    beside = beside + padded[1:-1, 2:, 1:-1] + padded[1:-1, :-2, 1:-1]
    beside = beside + padded[1:-1, 1:-1, 2:] + padded[1:-1, 1:-1, :-2]
    return beside - 6.0 * order_field


def relax_steps(order_field, others):
    for substep in range(SUBSTEPS):
        driving = growth_rate * order_field - quartic_rate * order_field * order_field * order_field
        driving = driving - 2.0 * coupling * order_field * others + gradient_energy * laplacian(order_field)
        order_field = order_field + time_step * driving
    return order_field


def reference(grain_boxes, box_anchors, migrations):
    grain_cubes = grain_boxes.reshape(BOXES, BOX, BOX, BOX)

    def deposit(box_index, grid_field):
        cube_field = lax.dynamic_index_in_dim(grain_cubes, box_index, 0, keepdims=False)
        anchor = lax.dynamic_index_in_dim(box_anchors, box_index, 0, keepdims=False)
        square = cube_field * cube_field
        placed = jnp.pad(square, ((0, 0), (0, TILE_YZ - BOX), (0, TILE_YZ - BOX)))
        placed = jnp.roll(placed, (anchor[1] * HALF, anchor[2] * HALF), axis=(1, 2))
        row_start = (anchor[0] * HALF).astype(jnp.int32)
        current = lax.dynamic_slice_in_dim(grid_field, row_start, BOX, 0)
        return lax.dynamic_update_slice_in_dim(grid_field, current + placed, row_start, 0)

    grid_field = jnp.zeros((NX + HALF, TILE_YZ, TILE_YZ), jnp.float32)
    grid_field = lax.fori_loop(0, BOXES, deposit, grid_field)
    covered = grid_field[:NX].at[:HALF].add(grid_field[NX:])
    extended = jnp.concatenate([covered, covered[:HALF]], axis=0)

    def relax_one(box_pair):
        cube_field, anchor = box_pair
        row_start = (anchor[0] * HALF).astype(jnp.int32)
        window = lax.dynamic_slice_in_dim(extended, row_start, BOX, 0)
        window = jnp.roll(window, (-anchor[1] * HALF, -anchor[2] * HALF), axis=(1, 2))[:, :BOX, :BOX]
        others = window - cube_field * cube_field
        return relax_steps(cube_field, others).reshape(BOX, BOX * BOX)

    relaxed = lax.map(relax_one, (grain_cubes, box_anchors))
    grouped = relaxed.reshape(N_DEV, BOX_DEV, BOX, BOX * BOX)
    device_rows = jnp.arange(N_DEV, dtype=jnp.int32)
    rightward = jnp.roll(grouped[device_rows, migrations[:, 0]], 1, axis=0)
    leftward = jnp.roll(grouped[device_rows, migrations[:, 1]], -1, axis=0)
    grouped = grouped.at[device_rows, migrations[:, 0]].set(rightward)
    grouped = grouped.at[device_rows, migrations[:, 1]].set(leftward)
    return grouped.reshape(BOXES, BOX, BOX * BOX)
```

```python
import functools

import jax
import jax.numpy as jnp
from jax import lax
from jax.experimental import pallas as pl
from jax.experimental.pallas import tpu as pltpu
from jax.sharding import PartitionSpec as P

SUBSTEPS = 4

growth_rate = 1.0
quartic_rate = 1.0
coupling = 1.5
gradient_energy = 2.0
time_step = 0.02

LANES = 128


def from_outward(value, steps):
    count = lax.axis_size("dev")
    pairs = []
    for target in range(count):
        outward = 1 if target % 2 else -1
        pairs.append(((target + outward * steps) % count, target))
    return lax.ppermute(value, "dev", pairs)


def add_squares(total_ref, box_ref, source, target, grid_tiles, skip=None, halves=(0, 1)):
    half = box_ref.shape[0] // 2
    area_half = box_ref.shape[1] // 2
    edge = 2 * half
    delta_x = lax.rem(source[0] - target[0] + grid_tiles + grid_tiles // 2, grid_tiles)
    delta_x = delta_x - grid_tiles // 2
    delta_y = lax.rem(source[1] - target[1] + 4, 4)
    delta_z = lax.rem(source[2] - target[2] + 4, 4)
    meets = (delta_x >= -1) & (delta_x <= 1) & (delta_y != 2) & (delta_z != 2)
    if skip is not None:
        meets = meets & jnp.logical_not(skip)

    @pl.when(meets)
    def _():
        lane = lax.broadcasted_iota(jnp.int32, (half, LANES), 1) % edge
        first = jnp.where(delta_z == 1, half, 0)
        final = jnp.where(delta_z == 3, half, edge)
        inside = (lane >= first) & (lane < final)
        shift = delta_z * half
        for half_x in halves:
            from_x = half_x - delta_x
            row_out = (half_x - halves[0]) * half
            for half_y in range(2):
                from_y = lax.rem(half_y - delta_y + 4, 4)

                @pl.when((from_x >= 0) & (from_x <= 1) & (from_y <= 1))
                def _():
                    row = pl.multiple_of(from_x * half, half)

                    def chunk(at, carry):
                        column = pl.multiple_of(from_y * area_half + at * LANES, LANES)
                        out = pl.multiple_of(half_y * area_half + at * LANES, LANES)
                        value = box_ref[pl.ds(row, half), pl.ds(column, LANES)]
                        value = pltpu.roll(value * value, shift, 1)
                        value = jnp.where(inside, value, 0.0)
                        total_ref[row_out : row_out + half, pl.ds(out, LANES)] += value
                        return carry

                    lax.fori_loop(0, area_half // LANES, chunk, 0, unroll=4)


def box_anchor(meta_ref, row, slot):
    return [meta_ref[row, slot * 3 + axis] for axis in range(3)]


def partial_kernel(grid_tiles, meta_ref, own_ref, partner_ref, full_ref, near_ref):
    outward = meta_ref[0, 8]
    slot_full = jnp.where(outward == 1, meta_ref[2, 6], meta_ref[2, 7])
    slot_near = jnp.where(outward == 1, meta_ref[3, 6], meta_ref[3, 7])
    target_full = box_anchor(meta_ref, 2, slot_full)
    target_near = box_anchor(meta_ref, 3, slot_near)
    full_ref[...] = jnp.zeros_like(full_ref)
    near_ref[...] = jnp.zeros_like(near_ref)
    for box in range(2):
        own = box_anchor(meta_ref, 0, box)
        partner = box_anchor(meta_ref, 1, box)
        add_squares(full_ref, own_ref.at[box], own, target_full, grid_tiles)
        add_squares(full_ref, partner_ref.at[box], partner, target_full, grid_tiles)
        for side in range(2):

            @pl.when(outward == 1 - side)
            def _(side=side, own=own, box=box):
                add_squares(near_ref, own_ref.at[box], own, target_near, grid_tiles, halves=(side,))


def relax_into(order_refs, factor_ref, out_ref, edge):
    rows, area = factor_ref.shape
    chunks = area // LANES
    lane = lax.broadcasted_iota(jnp.int32, (rows, LANES), 1)
    row = lax.broadcasted_iota(jnp.int32, (rows, LANES), 0)
    low_half = lane < edge
    at_z_end = lane % edge == edge - 1
    at_z_start = lane % edge == 0
    at_x_end = row == rows - 1
    at_x_start = row == 0
    for substep in range(SUBSTEPS):
        source = order_refs[substep % 2]
        target = order_refs[(substep + 1) % 2]
        final = substep == SUBSTEPS - 1

        def chunk(at, carry, source=source, target=target, final=final):
            swapped_before, swapped, order = carry
            start = pl.multiple_of(at * LANES, LANES)
            after = source[:, pl.ds(pl.multiple_of(start + 2 * LANES, LANES), LANES)]
            swapped_after = pltpu.roll(after, edge, 1)
            factor = factor_ref[:, pl.ds(start, LANES)]
            beside = jnp.where(low_half, swapped, swapped_after)
            beside += jnp.where(low_half, swapped_before, swapped)
            beside += jnp.where(at_z_end, 0.0, pltpu.roll(order, LANES - 1, 1))
            beside += jnp.where(at_z_start, 0.0, pltpu.roll(order, 1, 1))
            beside += jnp.where(at_x_end, 0.0, pltpu.roll(order, rows - 1, 0))
            beside += jnp.where(at_x_start, 0.0, pltpu.roll(order, 1, 0))
            relaxed = order * (factor - (time_step * quartic_rate) * (order * order))
            relaxed += (time_step * gradient_energy) * beside
            if final:
                out_ref[:, pl.ds(start, LANES)] = relaxed
            else:
                target[:, pl.ds(pl.multiple_of(start + LANES, LANES), LANES)] = relaxed
            return swapped, swapped_after, after

        first = source[:, pl.ds(LANES, LANES)]
        zeros = jnp.zeros((rows, LANES), jnp.float32)
        lax.fori_loop(0, chunks, chunk, (zeros, pltpu.roll(first, edge, 1), first), unroll=2)


def final_kernel(
    grid_tiles,
    meta_ref,
    own_ref,
    partner_ref,
    outer_ref,
    outer2_ref,
    inner2_ref,
    inner3_ref,
    full_ref,
    near_ref,
    out_ref,
    order_a,
    order_b,
    total_ref,
):
    rows, area = total_ref.shape
    edge = rows
    half = rows // 2
    outward = meta_ref[0, 8]
    sources = [own_ref, partner_ref, outer_ref, outer2_ref, inner2_ref, inner3_ref]
    for order_ref in (order_a, order_b):
        order_ref[:, :LANES] = jnp.zeros((rows, LANES), jnp.float32)
        order_ref[:, area + LANES :] = jnp.zeros((rows, LANES), jnp.float32)
    for target_row in (1, 2):
        if target_row == 2:
            slot = jnp.where(outward == 1, meta_ref[2, 7], meta_ref[2, 6])
            out_slot = jnp.where(outward == 1, meta_ref[0, 7], meta_ref[0, 6])
            rows_met = (0, 1, 2, 3, 4)
            total_ref[...] = full_ref[...]
        else:
            slot = jnp.where(outward == 1, meta_ref[1, 6], meta_ref[1, 7])
            out_slot = jnp.where(outward == 1, meta_ref[0, 6], meta_ref[0, 7])
            rows_met = (0, 1, 2, 3, 4, 5)
            total_ref[...] = jnp.zeros_like(total_ref)
            near_row = pl.multiple_of((1 - outward) * half, half)
            total_ref[pl.ds(near_row, half), :] = near_ref[...]
        target = box_anchor(meta_ref, target_row, slot)
        for source_row in rows_met:
            box_refs = sources[source_row]

            def one_box(box, carry, box_refs=box_refs, source_row=source_row):
                source = box_anchor(meta_ref, source_row, box)
                skip = box == slot if source_row == target_row else None
                add_squares(total_ref, box_refs.at[box], source, target, grid_tiles, skip)
                return carry

            lax.fori_loop(0, 2, one_box, 0)
        base = 1.0 + time_step * (growth_rate - 6.0 * gradient_energy)
        total_ref[...] = base - (time_step * 2.0 * coupling) * total_ref[...]
        order_a[:, LANES : area + LANES] = sources[target_row][slot]
        relax_into((order_a, order_b), total_ref, out_ref.at[out_slot], edge)


def on_device(grain_boxes, box_anchors, migrations):
    box_count, box_edge, area = grain_boxes.shape
    devices = lax.axis_size("dev")
    position = lax.axis_index("dev")
    outward = (position % 2).astype(jnp.int32)
    meta = jnp.concatenate([box_anchors.reshape(1, -1), migrations.reshape(1, -1)], axis=1)
    partner = from_outward(grain_boxes, -1)
    outer = from_outward(grain_boxes, 1)
    outer2 = from_outward(grain_boxes, 2)
    meta_at = {steps: from_outward(meta, steps) for steps in (-1, 3, 2, 1, -2, -3)}
    meta_at[0] = meta

    def meta_rows(steps):
        rows = jnp.concatenate([meta_at[step] for step in steps], axis=0)
        flag = jnp.broadcast_to(outward.reshape(1, 1), (rows.shape[0], 1))
        return jnp.concatenate([rows, flag], axis=1)

    smem = pl.BlockSpec(memory_space=pltpu.SMEM)
    vmem = pl.BlockSpec(memory_space=pltpu.VMEM)
    half_shape = jax.ShapeDtypeStruct((box_edge // 2, area), jnp.float32)
    box_shape = jax.ShapeDtypeStruct((box_edge, area), jnp.float32)
    full_part, near_part = pl.pallas_call(
        functools.partial(partial_kernel, devices),
        out_shape=(box_shape, half_shape),
        in_specs=[smem, vmem, vmem],
        out_specs=(vmem, vmem),
        name="partial_windows",
        cost_estimate=pl.CostEstimate(flops=4_000_000, bytes_accessed=6_000_000, transcendentals=0),
    )(meta_rows((0, -1, 2, 3)), grain_boxes, partner)
    full_sum = from_outward(full_part, 3)
    near_sum = from_outward(near_part, -4)
    inner2 = from_outward(outer, -1)
    inner3 = from_outward(outer2, -1)
    padded = pltpu.VMEM((box_edge, area + 2 * LANES), jnp.float32)
    return pl.pallas_call(
        functools.partial(final_kernel, devices),
        out_shape=jax.ShapeDtypeStruct(grain_boxes.shape, jnp.float32),
        in_specs=[smem] + [vmem] * 8,
        out_specs=vmem,
        scratch_shapes=[padded, padded, pltpu.VMEM((box_edge, area), jnp.float32)],
        name="gather_and_relax",
        compiler_params=pltpu.CompilerParams(vmem_limit_bytes=40 * 1024 * 1024),
    )(
        meta_rows((0, -1, 1, 2, -2, -3)),
        grain_boxes,
        partner,
        outer,
        outer2,
        inner2,
        inner3,
        full_sum,
        near_sum,
    )


def solution(mesh):
    in_specs = (P("dev", None, None), P("dev", None), P("dev", None))
    out_specs = P("dev", None, None)
    return jax.shard_map(
        on_device, mesh=mesh, in_specs=in_specs, out_specs=out_specs, check_vma=False
    )
```

```python
import functools

import jax
import jax.numpy as jnp
from jax import lax
from jax.experimental import pallas as pl
from jax.experimental.pallas import tpu as pltpu
from jax.sharding import PartitionSpec as P


SUBSTEPS = 4

growth_rate = 1.0
quartic_rate = 1.0
coupling = 1.5
gradient_energy = 2.0
time_step = 0.02

LANES = 128


def from_outward(value, steps):
    count = lax.axis_size("dev")
    pairs = []
    for target in range(count):
        outward = 1 if target % 2 else -1
        pairs.append(((target + outward * steps) % count, target))
    return lax.ppermute(value, "dev", pairs)


def offsets_of(source, target, grid_tiles, skip=None):
    delta_x = lax.rem(source[0] - target[0] + grid_tiles + grid_tiles // 2, grid_tiles)
    delta_x = delta_x - grid_tiles // 2
    delta_y = lax.rem(source[1] - target[1] + 4, 4)
    delta_z = lax.rem(source[2] - target[2] + 4, 4)
    meets = (delta_x >= -1) & (delta_x <= 1) & (delta_y != 2) & (delta_z != 2)
    if skip is not None:
        meets = meets & jnp.logical_not(skip)
    return meets, delta_x, delta_y, delta_z


def add_squares(total_ref, box_ref, offsets, halves=(0, 1), ready=None):
    half = box_ref.shape[0] // 2
    area_half = box_ref.shape[1] // 2
    edge = 2 * half
    meets, delta_x, delta_y, delta_z = offsets

    @pl.when(meets)
    def _():
        if ready is not None:
            ready()
        lane = lax.broadcasted_iota(jnp.int32, (half, LANES), 1) % edge
        first = jnp.where(delta_z == 1, half, 0)
        final = jnp.where(delta_z == 3, half, edge)
        inside = (lane >= first) & (lane < final)
        shift = delta_z * half
        for half_x in halves:
            from_x = half_x - delta_x
            row_out = (half_x - halves[0]) * half
            for half_y in range(2):
                from_y = lax.rem(half_y - delta_y + 4, 4)

                @pl.when((from_x >= 0) & (from_x <= 1) & (from_y <= 1))
                def _():
                    row = pl.multiple_of(from_x * half, half)

                    def chunk(at, carry):
                        column = pl.multiple_of(from_y * area_half + at * LANES, LANES)
                        out = half_y * (area_half // LANES) + at
                        value = box_ref[pl.ds(row, half), pl.ds(column, LANES)]
                        value = pltpu.roll(value * value, shift, 1)
                        value = jnp.where(inside, value, 0.0)
                        total_ref[out, row_out : row_out + half, :] += value
                        return carry

                    lax.fori_loop(0, area_half // LANES, chunk, 0, unroll=4)


def box_anchor(meta_ref, row, slot):
    return [meta_ref[row, slot * 3 + axis] for axis in range(3)]


def target_slots(meta_ref, row):
    outward = meta_ref[0, 8]
    right = (outward == 1) == (row == 1)
    slot = jnp.where(right, meta_ref[row, 6], meta_ref[row, 7])
    out_slot = jnp.where(right, meta_ref[0, 6], meta_ref[0, 7])
    return slot, out_slot


def early_kernel(grid_tiles, meta_ref, own_ref, partner_ref, full_ref, near_ref, outer_ref, inner_ref):
    outward = meta_ref[0, 8]
    slot_full = jnp.where(outward == 1, meta_ref[3, 6], meta_ref[3, 7])
    slot_near = jnp.where(outward == 1, meta_ref[4, 6], meta_ref[4, 7])
    target_full = box_anchor(meta_ref, 3, slot_full)
    target_near = box_anchor(meta_ref, 4, slot_near)
    slot_outer = target_slots(meta_ref, 2)[0]
    slot_inner = target_slots(meta_ref, 1)[0]
    target_outer = box_anchor(meta_ref, 2, slot_outer)
    target_inner = box_anchor(meta_ref, 1, slot_inner)
    for total_ref in (full_ref, near_ref, outer_ref, inner_ref):
        total_ref[...] = jnp.zeros_like(total_ref)
    for row, refs in ((0, own_ref), (1, partner_ref)):

        def one_box(box, carry, row=row, refs=refs):
            anchor = box_anchor(meta_ref, row, box)
            box_ref = refs.at[box]
            skip = box == slot_inner if row == 1 else None
            add_squares(full_ref, box_ref, offsets_of(anchor, target_full, grid_tiles))
            add_squares(outer_ref, box_ref, offsets_of(anchor, target_outer, grid_tiles))
            add_squares(inner_ref, box_ref, offsets_of(anchor, target_inner, grid_tiles, skip))
            if row == 0:
                near = offsets_of(anchor, target_near, grid_tiles)
                for side in range(2):

                    @pl.when(outward == 1 - side)
                    def _(side=side):
                        add_squares(near_ref, box_ref, near, halves=(side,))

            return carry

        lax.fori_loop(0, 2, one_box, 0)


def relax_into(order_refs, factor_ref, out_ref, edge):
    chunks, rows, _ = factor_ref.shape
    groups = rows // 8
    lane = lax.broadcasted_iota(jnp.int32, (rows, LANES), 1)
    row = lax.broadcasted_iota(jnp.int32, (8, LANES), 0)
    low_half = lane < edge
    at_z_end = lane % edge == edge - 1
    at_z_start = lane % edge == 0
    for substep in range(SUBSTEPS):
        source = order_refs[substep % 2]
        target = order_refs[(substep + 1) % 2]
        final = substep == SUBSTEPS - 1

        def chunk(at, carry, source=source, target=target, final=final):
            swapped_before, swapped, order = carry
            after = source[at + 2]
            swapped_after = pltpu.roll(after, edge, 1)
            factor = factor_ref[at]
            beside = jnp.where(low_half, swapped, swapped_after)
            beside += jnp.where(low_half, swapped_before, swapped)
            beside += jnp.where(at_z_end, 0.0, pltpu.roll(order, LANES - 1, 1))
            beside += jnp.where(at_z_start, 0.0, pltpu.roll(order, 1, 1))
            upper = jnp.where(row == 7, 0.0, pltpu.roll(order[:8], 7, 0))
            lower = jnp.where(row == 0, 0.0, pltpu.roll(order[rows - 8 :], 1, 0))
            beside += jnp.concatenate([order[8:], upper], axis=0)
            beside += jnp.concatenate([lower, order[: rows - 8]], axis=0)
            relaxed = order * (factor - (time_step * quartic_rate) * (order * order))
            relaxed += (time_step * gradient_energy) * beside
            if final:
                for group in range(groups):
                    picked = pl.ds(group, groups, stride=groups)
                    out_ref.at[at][picked, :] = relaxed[group * 8 : group * 8 + 8]
            else:
                target[at + 1] = relaxed
            return swapped, swapped_after, after

        first = source[1]
        zeros = jnp.zeros((rows, LANES), jnp.float32)
        lax.fori_loop(0, chunks, chunk, (zeros, pltpu.roll(first, edge, 1), first), unroll=2)


def relax_kernel(grid_tiles, target_row, source_rows, aliased, *refs):
    meta_ref, total_in_ref, part_ref, target_ref = refs[:4]
    count = len(source_rows)
    source_refs = refs[4 : 4 + count]
    out_ref, order_a, order_b, total_ref, result_ref, stage, target_stage, sems = refs[
        4 + count + aliased :
    ]
    chunks, rows, _ = total_ref.shape
    half = rows // 2
    groups = rows // 8
    slot, out_slot = target_slots(meta_ref, target_row)
    target = box_anchor(meta_ref, target_row, slot)

    def fetch(at, carry):
        columns = pl.ds(pl.multiple_of(at * LANES, LANES), LANES)
        pltpu.make_async_copy(
            target_ref.at[slot, :, columns], target_stage.at[at], sems.at[2 * count]
        ).start()
        return carry

    lax.fori_loop(0, chunks, fetch, 0)
    work = []
    for place, source_row in enumerate(source_rows):
        for box in range(2):
            source = box_anchor(meta_ref, source_row, box)
            skip = slot == box if source_row == target_row else None
            offsets = offsets_of(source, target, grid_tiles, skip)
            at = 2 * place + box
            copy = pltpu.make_async_copy(source_refs[place].at[box], stage.at[at], sems.at[at])
            pl.when(offsets[0])(copy.start)
            work.append((at, offsets, copy))
    for order_ref in (order_a, order_b):
        order_ref[0] = jnp.zeros((rows, LANES), jnp.float32)
        order_ref[chunks + 1] = jnp.zeros((rows, LANES), jnp.float32)
    if target_row == 2:
        total_ref[...] = total_in_ref[...] + part_ref[...]
    else:
        total_ref[...] = total_in_ref[...]
        near_row = pl.multiple_of((1 - meta_ref[0, 8]) * half, half)
        total_ref[:, pl.ds(near_row, half), :] += part_ref[...]
    for at, offsets, copy in work:
        add_squares(total_ref, stage.at[at], offsets, ready=copy.wait)
    pltpu.make_async_copy(target_stage, target_stage, sems.at[2 * count]).wait()
    base = 1.0 + time_step * (growth_rate - 6.0 * gradient_energy)
    factor_ref = result_ref

    def prepare(at, carry):
        for group in range(groups):
            picked = pl.ds(group, groups, stride=groups)
            into = pl.ds(group * 8, 8)
            order_a[at + 1, into, :] = target_stage.at[at][picked, :]
            factor_ref[at, into, :] = (
                base - (time_step * 2.0 * coupling) * total_ref.at[at][picked, :]
            )
        return carry

    lax.fori_loop(0, chunks, prepare, 0, unroll=2)
    relax_into((order_a, order_b), factor_ref, total_ref, rows)

    def deliver(at, carry):
        columns = pl.ds(pl.multiple_of(at * LANES, LANES), LANES)
        pltpu.make_async_copy(
            total_ref.at[at], out_ref.at[out_slot, :, columns], sems.at[2 * count]
        ).start()
        return carry

    lax.fori_loop(0, chunks, deliver, 0)
    pltpu.make_async_copy(total_ref, total_ref, sems.at[2 * count]).wait()


def on_device(grain_boxes, box_anchors, migrations):
    _, box_edge, area = grain_boxes.shape
    devices = lax.axis_size("dev")
    position = lax.axis_index("dev")
    outward = (position % 2).astype(jnp.int32).reshape(1, 1)
    meta = jnp.concatenate([box_anchors.reshape(1, -1), migrations.reshape(1, -1)], axis=1)
    outer = from_outward(grain_boxes, 1)
    partner = from_outward(grain_boxes, -1)
    metas = [meta] + [from_outward(meta, steps) for steps in (-1, 1, 2, 3, -2, -3)]
    metas = jnp.concatenate(metas, axis=0)
    metas = jnp.concatenate([metas, jnp.broadcast_to(outward, (metas.shape[0], 1))], axis=1)

    smem = pl.BlockSpec(memory_space=pltpu.SMEM)
    vmem = pl.BlockSpec(memory_space=pltpu.VMEM)
    anywhere = pl.BlockSpec(memory_space=pl.ANY)
    chunks = area // LANES
    half_shape = jax.ShapeDtypeStruct((chunks, box_edge // 2, LANES), jnp.float32)
    box_shape = jax.ShapeDtypeStruct((chunks, box_edge, LANES), jnp.float32)
    full_part, near_part, outer_sum, inner_sum = pl.pallas_call(
        functools.partial(early_kernel, devices),
        out_shape=(box_shape, half_shape, box_shape, box_shape),
        in_specs=[smem, vmem, vmem],
        out_specs=(vmem,) * 4,
        name="early_sums",
        cost_estimate=pl.CostEstimate(flops=8_000_000, bytes_accessed=8_000_000, transcendentals=0),
    )(metas, grain_boxes, partner)
    full_sum = from_outward(full_part, 3)
    near_sum = from_outward(near_part, -4)
    later_boxes, outer = lax.optimization_barrier((grain_boxes, outer))
    outer2 = from_outward(later_boxes, 2)
    inner2 = from_outward(outer, -1)
    inner3 = from_outward(outer2, -1)

    def relax(target_row, source_rows, total, part, target_boxes, sources, before):
        count = len(source_rows)
        aliased = 0 if before is None else 1
        box_scratch = pltpu.VMEM((chunks, box_edge, LANES), jnp.float32)
        padded = pltpu.VMEM((chunks + 2, box_edge, LANES), jnp.float32)
        extra = () if before is None else (before,)
        return pl.pallas_call(
            functools.partial(relax_kernel, devices, target_row, source_rows, aliased),
            out_shape=jax.ShapeDtypeStruct(grain_boxes.shape, jnp.float32),
            in_specs=[smem, vmem, vmem] + [anywhere] * (1 + count + aliased),
            out_specs=anywhere,
            input_output_aliases={4 + count: 0} if aliased else {},
            scratch_shapes=[
                padded,
                padded,
                box_scratch,
                box_scratch,
                pltpu.VMEM((2 * count, box_edge, area), jnp.float32),
                box_scratch,
                pltpu.SemaphoreType.DMA((2 * count + 1,)),
            ],
            name="relax_outer" if target_row == 2 else "relax_inner",
            compiler_params=pltpu.CompilerParams(vmem_limit_bytes=32 * 1024 * 1024),
            cost_estimate=pl.CostEstimate(
                flops=20_000_000, bytes_accessed=10_000_000, transcendentals=0
            ),
        )(metas, total, part, target_boxes, *sources, *extra)

    first = relax(2, (2, 5, 3), outer_sum, full_sum, outer, (outer, inner2, outer2), None)
    return relax(
        1, (2, 5, 3, 6), inner_sum, near_sum, partner, (outer, inner2, outer2, inner3), first
    )


def solution(mesh):
    in_specs = (P("dev", None, None), P("dev", None), P("dev", None))
    out_specs = P("dev", None, None)
    return jax.shard_map(
        on_device, mesh=mesh, in_specs=in_specs, out_specs=out_specs, check_vma=False
    )
```

```python
import functools

import jax
import jax.numpy as jnp
from jax import lax
from jax.experimental import pallas as pl
from jax.experimental.pallas import tpu as pltpu
from jax.sharding import PartitionSpec as P


SUBSTEPS = 4

growth_rate = 1.0
quartic_rate = 1.0
coupling = 1.5
gradient_energy = 2.0
time_step = 0.02

LANES = 128


def from_outward(value, steps):
    count = lax.axis_size("dev")
    pairs = []
    for target in range(count):
        outward = 1 if target % 2 else -1
        pairs.append(((target + outward * steps) % count, target))
    return lax.ppermute(value, "dev", pairs)


def offsets_of(source, target, grid_tiles, skip=None):
    delta_x = lax.rem(source[0] - target[0] + grid_tiles + grid_tiles // 2, grid_tiles)
    delta_x = delta_x - grid_tiles // 2
    delta_y = lax.rem(source[1] - target[1] + 4, 4)
    delta_z = lax.rem(source[2] - target[2] + 4, 4)
    meets = (delta_x >= -1) & (delta_x <= 1) & (delta_y != 2) & (delta_z != 2)
    if skip is not None:
        meets = meets & jnp.logical_not(skip)
    return meets, delta_x, delta_y, delta_z


def add_squares(total_ref, box_ref, offsets, halves=(0, 1), ready=None):
    half = box_ref.shape[0] // 2
    area_half = box_ref.shape[1] // 2
    edge = 2 * half
    meets, delta_x, delta_y, delta_z = offsets

    @pl.when(meets)
    def _():
        if ready is not None:
            ready()
        lane = lax.broadcasted_iota(jnp.int32, (half, LANES), 1) % edge
        first = jnp.where(delta_z == 1, half, 0)
        final = jnp.where(delta_z == 3, half, edge)
        inside = (lane >= first) & (lane < final)
        shift = delta_z * half
        for half_x in halves:
            from_x = half_x - delta_x
            row_out = (half_x - halves[0]) * half
            for half_y in range(2):
                from_y = lax.rem(half_y - delta_y + 4, 4)

                @pl.when((from_x >= 0) & (from_x <= 1) & (from_y <= 1))
                def _():
                    row = pl.multiple_of(from_x * half, half)

                    def chunk(at, carry):
                        column = pl.multiple_of(from_y * area_half + at * LANES, LANES)
                        out = half_y * (area_half // LANES) + at
                        value = box_ref[pl.ds(row, half), pl.ds(column, LANES)]
                        value = pltpu.roll(value * value, shift, 1)
                        value = jnp.where(inside, value, 0.0)
                        total_ref[out, row_out : row_out + half, :] += value
                        return carry

                    lax.fori_loop(0, area_half // LANES, chunk, 0, unroll=4)


def box_anchor(meta_ref, row, slot):
    return [meta_ref[row, slot * 3 + axis] for axis in range(3)]


def target_slots(meta_ref, row):
    outward = meta_ref[0, 8]
    right = (outward == 1) == (row == 1)
    slot = jnp.where(right, meta_ref[row, 6], meta_ref[row, 7])
    out_slot = jnp.where(right, meta_ref[0, 6], meta_ref[0, 7])
    return slot, out_slot


def early_kernel(grid_tiles, meta_ref, own_ref, partner_ref, full_ref, near_ref, outer_ref, inner_ref):
    outward = meta_ref[0, 8]
    slot_full = jnp.where(outward == 1, meta_ref[3, 6], meta_ref[3, 7])
    slot_near = jnp.where(outward == 1, meta_ref[4, 6], meta_ref[4, 7])
    target_full = box_anchor(meta_ref, 3, slot_full)
    target_near = box_anchor(meta_ref, 4, slot_near)
    slot_outer = target_slots(meta_ref, 2)[0]
    slot_inner = target_slots(meta_ref, 1)[0]
    target_outer = box_anchor(meta_ref, 2, slot_outer)
    target_inner = box_anchor(meta_ref, 1, slot_inner)
    for total_ref in (full_ref, near_ref, outer_ref, inner_ref):
        total_ref[...] = jnp.zeros_like(total_ref)
    for row, refs in ((0, own_ref), (1, partner_ref)):

        def one_box(box, carry, row=row, refs=refs):
            anchor = box_anchor(meta_ref, row, box)
            box_ref = refs.at[box]
            skip = box == slot_inner if row == 1 else None
            add_squares(full_ref, box_ref, offsets_of(anchor, target_full, grid_tiles))
            add_squares(outer_ref, box_ref, offsets_of(anchor, target_outer, grid_tiles))
            add_squares(inner_ref, box_ref, offsets_of(anchor, target_inner, grid_tiles, skip))
            if row == 0:
                near = offsets_of(anchor, target_near, grid_tiles)
                for side in range(2):

                    @pl.when(outward == 1 - side)
                    def _(side=side):
                        add_squares(near_ref, box_ref, near, halves=(side,))

            return carry

        lax.fori_loop(0, 2, one_box, 0)


def relax_into(order_refs, factor_ref, out_ref, edge):
    chunks, rows, _ = factor_ref.shape
    groups = rows // 8
    lane = lax.broadcasted_iota(jnp.int32, (rows, LANES), 1)
    row = lax.broadcasted_iota(jnp.int32, (8, LANES), 0)
    low_half = lane < edge
    at_z_end = lane % edge == edge - 1
    at_z_start = lane % edge == 0
    for substep in range(SUBSTEPS):
        source = order_refs[substep % 2]
        target = order_refs[(substep + 1) % 2]
        final = substep == SUBSTEPS - 1

        def chunk(at, carry, source=source, target=target, final=final):
            swapped_before, swapped, order = carry
            after = source[at + 2]
            swapped_after = pltpu.roll(after, edge, 1)
            factor = factor_ref[at]
            beside = jnp.where(low_half, swapped, swapped_after)
            beside += jnp.where(low_half, swapped_before, swapped)
            beside += jnp.where(at_z_end, 0.0, pltpu.roll(order, LANES - 1, 1))
            beside += jnp.where(at_z_start, 0.0, pltpu.roll(order, 1, 1))
            upper = jnp.where(row == 7, 0.0, pltpu.roll(order[:8], 7, 0))
            lower = jnp.where(row == 0, 0.0, pltpu.roll(order[rows - 8 :], 1, 0))
            beside += jnp.concatenate([order[8:], upper], axis=0)
            beside += jnp.concatenate([lower, order[: rows - 8]], axis=0)
            relaxed = order * (factor - (time_step * quartic_rate) * (order * order))
            relaxed += (time_step * gradient_energy) * beside
            if final:
                for group in range(groups):
                    picked = pl.ds(group, groups, stride=groups)
                    out_ref.at[at][picked, :] = relaxed[group * 8 : group * 8 + 8]
            else:
                target[at + 1] = relaxed
            return swapped, swapped_after, after

        first = source[1]
        zeros = jnp.zeros((rows, LANES), jnp.float32)
        lax.fori_loop(0, chunks, chunk, (zeros, pltpu.roll(first, edge, 1), first), unroll=2)


def relax_kernel(grid_tiles, target_row, source_rows, aliased, *refs):
    meta_ref, total_in_ref, part_ref, target_ref = refs[:4]
    count = len(source_rows)
    source_refs = refs[4 : 4 + count]
    out_ref, order_a, order_b, total_ref, result_ref, stage, target_stage, sems = refs[
        4 + count + aliased :
    ]
    chunks, rows, _ = total_ref.shape
    half = rows // 2
    groups = rows // 8
    slot, out_slot = target_slots(meta_ref, target_row)
    target = box_anchor(meta_ref, target_row, slot)

    def fetch(at, carry):
        columns = pl.ds(pl.multiple_of(at * LANES, LANES), LANES)
        pltpu.make_async_copy(
            target_ref.at[slot, :, columns], target_stage.at[at], sems.at[2 * count]
        ).start()
        return carry

    lax.fori_loop(0, chunks, fetch, 0)
    work = []
    for place, source_row in enumerate(source_rows):
        for box in range(2):
            source = box_anchor(meta_ref, source_row, box)
            skip = slot == box if source_row == target_row else None
            offsets = offsets_of(source, target, grid_tiles, skip)
            at = 2 * place + box
            copy = pltpu.make_async_copy(source_refs[place].at[box], stage.at[at], sems.at[at])
            pl.when(offsets[0])(copy.start)
            work.append((at, offsets, copy))
    for order_ref in (order_a, order_b):
        order_ref[0] = jnp.zeros((rows, LANES), jnp.float32)
        order_ref[chunks + 1] = jnp.zeros((rows, LANES), jnp.float32)
    if target_row == 2:
        total_ref[...] = total_in_ref[...] + part_ref[...]
    else:
        total_ref[...] = total_in_ref[...]
        near_row = pl.multiple_of((1 - meta_ref[0, 8]) * half, half)
        total_ref[:, pl.ds(near_row, half), :] += part_ref[...]
    for at, offsets, copy in work:
        add_squares(total_ref, stage.at[at], offsets, ready=copy.wait)
    pltpu.make_async_copy(target_stage, target_stage, sems.at[2 * count]).wait()
    base = 1.0 + time_step * (growth_rate - 6.0 * gradient_energy)
    factor_ref = result_ref

    def prepare(at, carry):
        for group in range(groups):
            picked = pl.ds(group, groups, stride=groups)
            into = pl.ds(group * 8, 8)
            order_a[at + 1, into, :] = target_stage.at[at][picked, :]
            factor_ref[at, into, :] = (
                base - (time_step * 2.0 * coupling) * total_ref.at[at][picked, :]
            )
        return carry

    lax.fori_loop(0, chunks, prepare, 0, unroll=2)
    relax_into((order_a, order_b), factor_ref, total_ref, rows)

    def deliver(at, carry):
        columns = pl.ds(pl.multiple_of(at * LANES, LANES), LANES)
        pltpu.make_async_copy(
            total_ref.at[at], out_ref.at[out_slot, :, columns], sems.at[2 * count]
        ).start()
        return carry

    lax.fori_loop(0, chunks, deliver, 0)
    pltpu.make_async_copy(total_ref, total_ref, sems.at[2 * count]).wait()


def on_device(grain_boxes, box_anchors, migrations):
    _, box_edge, area = grain_boxes.shape
    devices = lax.axis_size("dev")
    position = lax.axis_index("dev")
    outward = (position % 2).astype(jnp.int32).reshape(1, 1)
    meta = jnp.concatenate([box_anchors.reshape(1, -1), migrations.reshape(1, -1)], axis=1)
    metas = [meta]
    for steps in (-1, 1, 2, 3):
        metas.append(from_outward(meta, steps))
    metas.append(from_outward(jnp.concatenate(metas[2:4], axis=0), -1))
    partner = from_outward(grain_boxes, -1)
    outer = from_outward(grain_boxes, 1)
    outer2 = from_outward(grain_boxes, 2)

    def with_flag(rows):
        rows = jnp.concatenate(rows, axis=0)
        return jnp.concatenate([rows, jnp.broadcast_to(outward, (rows.shape[0], 1))], axis=1)

    early_metas = with_flag(metas[:5])
    metas = with_flag(metas)

    smem = pl.BlockSpec(memory_space=pltpu.SMEM)
    vmem = pl.BlockSpec(memory_space=pltpu.VMEM)
    anywhere = pl.BlockSpec(memory_space=pl.ANY)
    chunks = area // LANES
    half_shape = jax.ShapeDtypeStruct((chunks, box_edge // 2, LANES), jnp.float32)
    box_shape = jax.ShapeDtypeStruct((chunks, box_edge, LANES), jnp.float32)
    full_part, near_part, outer_sum, inner_sum = pl.pallas_call(
        functools.partial(early_kernel, devices),
        out_shape=(box_shape, half_shape, box_shape, box_shape),
        in_specs=[smem, vmem, vmem],
        out_specs=(vmem,) * 4,
        name="early_sums",
        cost_estimate=pl.CostEstimate(flops=8_000_000, bytes_accessed=8_000_000, transcendentals=0),
    )(early_metas, grain_boxes, partner)
    full_sum = from_outward(full_part, 3)
    near_sum = from_outward(near_part, -4)
    inner2 = from_outward(outer, -1)
    inner3 = from_outward(outer2, -1)

    def relax(target_row, source_rows, total, part, target_boxes, sources, before):
        count = len(source_rows)
        aliased = 0 if before is None else 1
        box_scratch = pltpu.VMEM((chunks, box_edge, LANES), jnp.float32)
        padded = pltpu.VMEM((chunks + 2, box_edge, LANES), jnp.float32)
        extra = () if before is None else (before,)
        return pl.pallas_call(
            functools.partial(relax_kernel, devices, target_row, source_rows, aliased),
            out_shape=jax.ShapeDtypeStruct(grain_boxes.shape, jnp.float32),
            in_specs=[smem, vmem, vmem] + [anywhere] * (1 + count + aliased),
            out_specs=anywhere,
            input_output_aliases={4 + count: 0} if aliased else {},
            scratch_shapes=[
                padded,
                padded,
                box_scratch,
                box_scratch,
                pltpu.VMEM((2 * count, box_edge, area), jnp.float32),
                box_scratch,
                pltpu.SemaphoreType.DMA((2 * count + 1,)),
            ],
            name="relax_outer" if target_row == 2 else "relax_inner",
            compiler_params=pltpu.CompilerParams(vmem_limit_bytes=32 * 1024 * 1024),
            cost_estimate=pl.CostEstimate(
                flops=20_000_000, bytes_accessed=10_000_000, transcendentals=0
            ),
        )(metas, total, part, target_boxes, *sources, *extra)

    first = relax(2, (2, 5, 3), outer_sum, full_sum, outer, (outer, inner2, outer2), None)
    return relax(
        1, (2, 5, 3, 6), inner_sum, near_sum, partner, (outer, inner2, outer2, inner3), first
    )


def solution(mesh):
    in_specs = (P("dev", None, None), P("dev", None), P("dev", None))
    out_specs = P("dev", None, None)
    return jax.shard_map(
        on_device, mesh=mesh, in_specs=in_specs, out_specs=out_specs, check_vma=False
    )
```

```python
import functools

import jax
import jax.numpy as jnp
from jax import lax
from jax.experimental import pallas as pl
from jax.experimental.pallas import tpu as pltpu
from jax.sharding import PartitionSpec as P


SUBSTEPS = 4

growth_rate = 1.0
quartic_rate = 1.0
coupling = 1.5
gradient_energy = 2.0
time_step = 0.02

LANES = 128


def from_outward(value, steps):
    count = lax.axis_size("dev")
    pairs = []
    for target in range(count):
        outward = 1 if target % 2 else -1
        pairs.append(((target + outward * steps) % count, target))
    return lax.ppermute(value, "dev", pairs)


def offsets_of(source, target, grid_tiles, skip=None):
    delta_x = lax.rem(source[0] - target[0] + grid_tiles + grid_tiles // 2, grid_tiles)
    delta_x = delta_x - grid_tiles // 2
    delta_y = lax.rem(source[1] - target[1] + 4, 4)
    delta_z = lax.rem(source[2] - target[2] + 4, 4)
    meets = (delta_x >= -1) & (delta_x <= 1) & (delta_y != 2) & (delta_z != 2)
    if skip is not None:
        meets = meets & jnp.logical_not(skip)
    return meets, delta_x, delta_y, delta_z


def add_squares(total_ref, box_ref, offsets, halves=(0, 1), ready=None):
    half = box_ref.shape[0] // 2
    area_half = box_ref.shape[1] // 2
    edge = 2 * half
    meets, delta_x, delta_y, delta_z = offsets

    @pl.when(meets)
    def _():
        if ready is not None:
            ready()
        lane = lax.broadcasted_iota(jnp.int32, (half, LANES), 1) % edge
        first = jnp.where(delta_z == 1, half, 0)
        final = jnp.where(delta_z == 3, half, edge)
        inside = (lane >= first) & (lane < final)
        shift = delta_z * half
        for half_x in halves:
            from_x = half_x - delta_x
            row_out = (half_x - halves[0]) * half
            for half_y in range(2):
                from_y = lax.rem(half_y - delta_y + 4, 4)

                @pl.when((from_x >= 0) & (from_x <= 1) & (from_y <= 1))
                def _():
                    row = pl.multiple_of(from_x * half, half)

                    def chunk(at, carry):
                        column = pl.multiple_of(from_y * area_half + at * LANES, LANES)
                        out = half_y * (area_half // LANES) + at
                        value = box_ref[pl.ds(row, half), pl.ds(column, LANES)]
                        value = pltpu.roll(value * value, shift, 1)
                        value = jnp.where(inside, value, 0.0)
                        total_ref[out, row_out : row_out + half, :] += value
                        return carry

                    lax.fori_loop(0, area_half // LANES, chunk, 0, unroll=4)


def box_anchor(meta_ref, row, slot):
    return [meta_ref[row, slot * 3 + axis] for axis in range(3)]


def target_slots(meta_ref, row):
    outward = meta_ref[0, 8]
    right = (outward == 1) == (row == 1)
    slot = jnp.where(right, meta_ref[row, 6], meta_ref[row, 7])
    out_slot = jnp.where(right, meta_ref[0, 6], meta_ref[0, 7])
    return slot, out_slot


def early_kernel(grid_tiles, meta_ref, own_ref, partner_ref, full_ref, near_ref, outer_ref, inner_ref):
    outward = meta_ref[0, 8]
    slot_full = jnp.where(outward == 1, meta_ref[3, 6], meta_ref[3, 7])
    slot_near = jnp.where(outward == 1, meta_ref[4, 6], meta_ref[4, 7])
    target_full = box_anchor(meta_ref, 3, slot_full)
    target_near = box_anchor(meta_ref, 4, slot_near)
    slot_outer = target_slots(meta_ref, 2)[0]
    slot_inner = target_slots(meta_ref, 1)[0]
    target_outer = box_anchor(meta_ref, 2, slot_outer)
    target_inner = box_anchor(meta_ref, 1, slot_inner)
    for total_ref in (full_ref, near_ref, outer_ref, inner_ref):
        total_ref[...] = jnp.zeros_like(total_ref)
    for row, refs in ((0, own_ref), (1, partner_ref)):

        def one_box(box, carry, row=row, refs=refs):
            anchor = box_anchor(meta_ref, row, box)
            box_ref = refs.at[box]
            skip = box == slot_inner if row == 1 else None
            add_squares(full_ref, box_ref, offsets_of(anchor, target_full, grid_tiles))
            add_squares(outer_ref, box_ref, offsets_of(anchor, target_outer, grid_tiles))
            add_squares(inner_ref, box_ref, offsets_of(anchor, target_inner, grid_tiles, skip))
            if row == 0:
                near = offsets_of(anchor, target_near, grid_tiles)
                for side in range(2):

                    @pl.when(outward == 1 - side)
                    def _(side=side):
                        add_squares(near_ref, box_ref, near, halves=(side,))

            return carry

        lax.fori_loop(0, 2, one_box, 0)


def relax_into(order_refs, factor_ref, edge):
    chunks, rows, _ = factor_ref.shape
    lane = lax.broadcasted_iota(jnp.int32, (rows, LANES), 1)
    row = lax.broadcasted_iota(jnp.int32, (8, LANES), 0)
    low_half = lane < edge
    at_z_end = lane % edge == edge - 1
    at_z_start = lane % edge == 0
    for substep in range(SUBSTEPS):
        source = order_refs[substep % 2]
        target = order_refs[(substep + 1) % 2]
        source[0] = jnp.where(low_half, 0.0, pltpu.roll(source[chunks], edge, 1))
        source[chunks + 1] = jnp.where(low_half, pltpu.roll(source[1], edge, 1), 0.0)

        def chunk(at, carry, source=source, target=target):
            before, order = carry
            after = source[at + 2]
            factor = factor_ref[at]
            beside = before + after
            beside += jnp.where(at_z_end, 0.0, pltpu.roll(order, LANES - 1, 1))
            beside += jnp.where(at_z_start, 0.0, pltpu.roll(order, 1, 1))
            upper = jnp.where(row == 7, 0.0, pltpu.roll(order[:8], 7, 0))
            lower = jnp.where(row == 0, 0.0, pltpu.roll(order[rows - 8 :], 1, 0))
            beside += jnp.concatenate([order[8:], upper], axis=0)
            beside += jnp.concatenate([lower, order[: rows - 8]], axis=0)
            relaxed = order * (factor - (time_step * quartic_rate) * (order * order))
            target[at + 1] = relaxed + (time_step * gradient_energy) * beside
            return order, after

        lax.fori_loop(0, chunks, chunk, (source[0], source[1]), unroll=2)


def relax_kernel(grid_tiles, target_row, source_rows, aliased, *refs):
    meta_ref, total_in_ref, part_ref, target_ref = refs[:4]
    count = len(source_rows)
    source_refs = refs[4 : 4 + count]
    out_ref, order_a, order_b, total_ref, result_ref, stage, target_stage, sems = refs[
        4 + count + aliased :
    ]
    chunks, rows, _ = total_ref.shape
    half = rows // 2
    groups = rows // 8
    slot, out_slot = target_slots(meta_ref, target_row)
    target = box_anchor(meta_ref, target_row, slot)

    def fetch(at, carry):
        columns = pl.ds(pl.multiple_of(at * LANES, LANES), LANES)
        pltpu.make_async_copy(
            target_ref.at[slot, :, columns], target_stage.at[at], sems.at[2 * count]
        ).start()
        return carry

    lax.fori_loop(0, chunks, fetch, 0)
    work = []
    for place, source_row in enumerate(source_rows):
        for box in range(2):
            source = box_anchor(meta_ref, source_row, box)
            skip = slot == box if source_row == target_row else None
            offsets = offsets_of(source, target, grid_tiles, skip)
            at = 2 * place + box
            copy = pltpu.make_async_copy(source_refs[place].at[box], stage.at[at], sems.at[at])
            pl.when(offsets[0])(copy.start)
            work.append((at, offsets, copy))
    if target_row == 2:
        total_ref[...] = total_in_ref[...] + part_ref[...]
    else:
        total_ref[...] = total_in_ref[...]
        near_row = pl.multiple_of((1 - meta_ref[0, 8]) * half, half)
        total_ref[:, pl.ds(near_row, half), :] += part_ref[...]
    for at, offsets, copy in work:
        add_squares(total_ref, stage.at[at], offsets, ready=copy.wait)
    pltpu.make_async_copy(target_stage, target_stage, sems.at[2 * count]).wait()
    base = 1.0 + time_step * (growth_rate - 6.0 * gradient_energy)
    factor_ref = result_ref

    low_half = lax.broadcasted_iota(jnp.int32, (8, LANES), 1) < rows
    pairs = chunks // 2

    def interleave(first, second):
        even = jnp.where(low_half, first, pltpu.roll(second, rows, 1))
        odd = jnp.where(low_half, pltpu.roll(first, rows, 1), second)
        return even, odd

    def prepare(at, carry):
        for group in range(groups):
            picked = pl.ds(group, groups, stride=groups)
            into = pl.ds(group * 8, 8)
            even, odd = interleave(
                target_stage.at[at][picked, :], target_stage.at[at + pairs][picked, :]
            )
            order_a[2 * at + 1, into, :] = even
            order_a[2 * at + 2, into, :] = odd
            even, odd = interleave(total_ref.at[at][picked, :], total_ref.at[at + pairs][picked, :])
            factor_ref[2 * at, into, :] = base - (time_step * 2.0 * coupling) * even
            factor_ref[2 * at + 1, into, :] = base - (time_step * 2.0 * coupling) * odd
        return carry

    lax.fori_loop(0, pairs, prepare, 0)
    orders = (order_a, order_b)
    relax_into(orders, factor_ref, rows)
    relaxed_ref = orders[SUBSTEPS % 2]

    def deliver(at, carry):
        for group in range(groups):
            picked = pl.ds(group, groups, stride=groups)
            even = relaxed_ref[2 * at + 1, group * 8 : group * 8 + 8, :]
            odd = relaxed_ref[2 * at + 2, group * 8 : group * 8 + 8, :]
            total_ref.at[at][picked, :] = jnp.where(low_half, even, pltpu.roll(odd, rows, 1))
            total_ref.at[at + pairs][picked, :] = jnp.where(
                low_half, pltpu.roll(even, rows, 1), odd
            )
        for chunk in (at, at + pairs):
            columns = pl.ds(pl.multiple_of(chunk * LANES, LANES), LANES)
            pltpu.make_async_copy(
                total_ref.at[chunk], out_ref.at[out_slot, :, columns], sems.at[2 * count]
            ).start()
        return carry

    lax.fori_loop(0, pairs, deliver, 0)
    pltpu.make_async_copy(total_ref, total_ref, sems.at[2 * count]).wait()


def on_device(grain_boxes, box_anchors, migrations):
    _, box_edge, area = grain_boxes.shape
    devices = lax.axis_size("dev")
    position = lax.axis_index("dev")
    outward = (position % 2).astype(jnp.int32).reshape(1, 1)
    meta = jnp.concatenate([box_anchors.reshape(1, -1), migrations.reshape(1, -1)], axis=1)
    metas = [meta]
    for steps in (-1, 1, 2, 3):
        metas.append(from_outward(meta, steps))
    metas.append(from_outward(jnp.concatenate(metas[2:4], axis=0), -1))
    partner = from_outward(grain_boxes, -1)
    outer = from_outward(grain_boxes, 1)
    outer2 = from_outward(grain_boxes, 2)

    def with_flag(rows):
        rows = jnp.concatenate(rows, axis=0)
        return jnp.concatenate([rows, jnp.broadcast_to(outward, (rows.shape[0], 1))], axis=1)

    early_metas = with_flag(metas[:5])
    metas = with_flag(metas)

    smem = pl.BlockSpec(memory_space=pltpu.SMEM)
    vmem = pl.BlockSpec(memory_space=pltpu.VMEM)
    anywhere = pl.BlockSpec(memory_space=pl.ANY)
    chunks = area // LANES
    half_shape = jax.ShapeDtypeStruct((chunks, box_edge // 2, LANES), jnp.float32)
    box_shape = jax.ShapeDtypeStruct((chunks, box_edge, LANES), jnp.float32)
    full_part, near_part, outer_sum, inner_sum = pl.pallas_call(
        functools.partial(early_kernel, devices),
        out_shape=(box_shape, half_shape, box_shape, box_shape),
        in_specs=[smem, vmem, vmem],
        out_specs=(vmem,) * 4,
        name="early_sums",
        cost_estimate=pl.CostEstimate(flops=8_000_000, bytes_accessed=8_000_000, transcendentals=0),
    )(early_metas, grain_boxes, partner)
    full_sum = from_outward(full_part, 3)
    near_sum = from_outward(near_part, -4)
    inner2 = from_outward(outer, -1)
    inner3 = from_outward(outer2, -1)

    def relax(target_row, source_rows, total, part, target_boxes, sources, before):
        count = len(source_rows)
        aliased = 0 if before is None else 1
        box_scratch = pltpu.VMEM((chunks, box_edge, LANES), jnp.float32)
        padded = pltpu.VMEM((chunks + 2, box_edge, LANES), jnp.float32)
        extra = () if before is None else (before,)
        return pl.pallas_call(
            functools.partial(relax_kernel, devices, target_row, source_rows, aliased),
            out_shape=jax.ShapeDtypeStruct(grain_boxes.shape, jnp.float32),
            in_specs=[smem, vmem, vmem] + [anywhere] * (1 + count + aliased),
            out_specs=anywhere,
            input_output_aliases={4 + count: 0} if aliased else {},
            scratch_shapes=[
                padded,
                padded,
                box_scratch,
                box_scratch,
                pltpu.VMEM((2 * count, box_edge, area), jnp.float32),
                box_scratch,
                pltpu.SemaphoreType.DMA((2 * count + 1,)),
            ],
            name="relax_outer" if target_row == 2 else "relax_inner",
            compiler_params=pltpu.CompilerParams(vmem_limit_bytes=32 * 1024 * 1024),
            cost_estimate=pl.CostEstimate(
                flops=20_000_000, bytes_accessed=10_000_000, transcendentals=0
            ),
        )(metas, total, part, target_boxes, *sources, *extra)

    first = relax(2, (2, 5, 3), outer_sum, full_sum, outer, (outer, inner2, outer2), None)
    return relax(
        1, (2, 5, 3, 6), inner_sum, near_sum, partner, (outer, inner2, outer2, inner3), first
    )


def solution(mesh):
    in_specs = (P("dev", None, None), P("dev", None), P("dev", None))
    out_specs = P("dev", None, None)
    return jax.shard_map(
        on_device, mesh=mesh, in_specs=in_specs, out_specs=out_specs, check_vma=False
    )
```

```python
import functools

import jax
import jax.numpy as jnp
from jax import lax
from jax.experimental import pallas as pl
from jax.experimental.pallas import tpu as pltpu
from jax.sharding import PartitionSpec as P


SUBSTEPS = 4

growth_rate = 1.0
quartic_rate = 1.0
coupling = 1.5
gradient_energy = 2.0
time_step = 0.02

LANES = 128


def from_outward(value, steps):
    count = lax.axis_size("dev")
    pairs = []
    for target in range(count):
        outward = 1 if target % 2 else -1
        pairs.append(((target + outward * steps) % count, target))
    return lax.ppermute(value, "dev", pairs)


def offsets_of(source, target, grid_tiles, skip=None):
    delta_x = lax.rem(source[0] - target[0] + grid_tiles + grid_tiles // 2, grid_tiles)
    delta_x = delta_x - grid_tiles // 2
    delta_y = lax.rem(source[1] - target[1] + 4, 4)
    delta_z = lax.rem(source[2] - target[2] + 4, 4)
    meets = (delta_x >= -1) & (delta_x <= 1) & (delta_y != 2) & (delta_z != 2)
    if skip is not None:
        meets = meets & jnp.logical_not(skip)
    return meets, delta_x, delta_y, delta_z


def add_squares(total_ref, box_ref, offsets, halves=(0, 1), ready=None):
    half = box_ref.shape[0] // 2
    area_half = box_ref.shape[1] // 2
    edge = 2 * half
    meets, delta_x, delta_y, delta_z = offsets

    @pl.when(meets)
    def _():
        if ready is not None:
            ready()
        lane = lax.broadcasted_iota(jnp.int32, (half, LANES), 1) % edge
        first = jnp.where(delta_z == 1, half, 0)
        final = jnp.where(delta_z == 3, half, edge)
        inside = (lane >= first) & (lane < final)
        shift = delta_z * half
        for half_x in halves:
            from_x = half_x - delta_x
            row_out = (half_x - halves[0]) * half
            for half_y in range(2):
                from_y = lax.rem(half_y - delta_y + 4, 4)

                @pl.when((from_x >= 0) & (from_x <= 1) & (from_y <= 1))
                def _():
                    row = pl.multiple_of(from_x * half, half)

                    def chunk(at, carry):
                        column = pl.multiple_of(from_y * area_half + at * LANES, LANES)
                        out = half_y * (area_half // LANES) + at
                        value = box_ref[pl.ds(row, half), pl.ds(column, LANES)]
                        value = pltpu.roll(value * value, shift, 1)
                        value = jnp.where(inside, value, 0.0)
                        total_ref[out, row_out : row_out + half, :] += value
                        return carry

                    lax.fori_loop(0, area_half // LANES, chunk, 0, unroll=4)


def box_anchor(meta_ref, row, slot):
    return [meta_ref[row, slot * 3 + axis] for axis in range(3)]


def target_slots(meta_ref, row):
    outward = meta_ref[0, 8]
    right = (outward == 1) == (row == 1)
    slot = jnp.where(right, meta_ref[row, 6], meta_ref[row, 7])
    out_slot = jnp.where(right, meta_ref[0, 6], meta_ref[0, 7])
    return slot, out_slot


def early_kernel(grid_tiles, meta_ref, own_ref, partner_ref, full_ref, near_ref, outer_ref, inner_ref):
    outward = meta_ref[0, 8]
    slot_full = jnp.where(outward == 1, meta_ref[3, 6], meta_ref[3, 7])
    slot_near = jnp.where(outward == 1, meta_ref[4, 6], meta_ref[4, 7])
    target_full = box_anchor(meta_ref, 3, slot_full)
    target_near = box_anchor(meta_ref, 4, slot_near)
    slot_outer = target_slots(meta_ref, 2)[0]
    slot_inner = target_slots(meta_ref, 1)[0]
    target_outer = box_anchor(meta_ref, 2, slot_outer)
    target_inner = box_anchor(meta_ref, 1, slot_inner)
    for total_ref in (full_ref, near_ref, outer_ref, inner_ref):
        total_ref[...] = jnp.zeros_like(total_ref)
    for row, refs in ((0, own_ref), (1, partner_ref)):

        def one_box(box, carry, row=row, refs=refs):
            anchor = box_anchor(meta_ref, row, box)
            box_ref = refs.at[box]
            skip = box == slot_inner if row == 1 else None
            add_squares(full_ref, box_ref, offsets_of(anchor, target_full, grid_tiles))
            add_squares(outer_ref, box_ref, offsets_of(anchor, target_outer, grid_tiles))
            add_squares(inner_ref, box_ref, offsets_of(anchor, target_inner, grid_tiles, skip))
            if row == 0:
                near = offsets_of(anchor, target_near, grid_tiles)
                for side in range(2):

                    @pl.when(outward == 1 - side)
                    def _(side=side):
                        add_squares(near_ref, box_ref, near, halves=(side,))

            return carry

        lax.fori_loop(0, 2, one_box, 0)


def relax_into(order_refs, factor_ref, out_ref, edge, deliver):
    chunks, rows, _ = factor_ref.shape
    groups = rows // 8
    lane = lax.broadcasted_iota(jnp.int32, (rows, LANES), 1)
    row = lax.broadcasted_iota(jnp.int32, (8, LANES), 0)
    low_half = lane < edge
    at_z_end = lane % edge == edge - 1
    at_z_start = lane % edge == 0
    for substep in range(SUBSTEPS):
        source = order_refs[substep % 2]
        target = order_refs[(substep + 1) % 2]
        final = substep == SUBSTEPS - 1

        def chunk(at, carry, source=source, target=target, final=final):
            swapped_before, swapped, order = carry
            after = source[at + 2]
            swapped_after = pltpu.roll(after, edge, 1)
            factor = factor_ref[at]
            beside = jnp.where(low_half, swapped, swapped_after)
            beside += jnp.where(low_half, swapped_before, swapped)
            beside += jnp.where(at_z_end, 0.0, pltpu.roll(order, LANES - 1, 1))
            beside += jnp.where(at_z_start, 0.0, pltpu.roll(order, 1, 1))
            upper = jnp.where(row == 7, 0.0, pltpu.roll(order[:8], 7, 0))
            lower = jnp.where(row == 0, 0.0, pltpu.roll(order[rows - 8 :], 1, 0))
            beside += jnp.concatenate([order[8:], upper], axis=0)
            beside += jnp.concatenate([lower, order[: rows - 8]], axis=0)
            relaxed = order * (factor - (time_step * quartic_rate) * (order * order))
            relaxed += (time_step * gradient_energy) * beside
            if final:
                for group in range(groups):
                    picked = pl.ds(group, groups, stride=groups)
                    out_ref.at[at][picked, :] = relaxed[group * 8 : group * 8 + 8]
                deliver(at)
            else:
                target[at + 1] = relaxed
            return swapped, swapped_after, after

        first = source[1]
        zeros = jnp.zeros((rows, LANES), jnp.float32)
        lax.fori_loop(0, chunks, chunk, (zeros, pltpu.roll(first, edge, 1), first), unroll=2)


def relax_kernel(grid_tiles, target_row, source_rows, aliased, *refs):
    meta_ref, total_in_ref, part_ref, target_ref = refs[:4]
    count = len(source_rows)
    source_refs = refs[4 : 4 + count]
    out_ref, order_a, order_b, total_ref, result_ref, stage, target_stage, part_stage, sems = refs[
        4 + count + aliased :
    ]
    chunks, rows, _ = total_ref.shape
    half = rows // 2
    groups = rows // 8
    slot, out_slot = target_slots(meta_ref, target_row)
    target = box_anchor(meta_ref, target_row, slot)

    total_copy = pltpu.make_async_copy(total_in_ref, total_ref, sems.at[2 * count + 1])
    total_copy.start()
    part_copy = pltpu.make_async_copy(part_ref, part_stage, sems.at[2 * count + 2])
    part_copy.start()

    def fetch(at, carry):
        columns = pl.ds(pl.multiple_of(at * LANES, LANES), LANES)
        pltpu.make_async_copy(
            target_ref.at[slot, :, columns], target_stage.at[at], sems.at[2 * count]
        ).start()
        return carry

    lax.fori_loop(0, chunks, fetch, 0)
    work = []
    for place, source_row in enumerate(source_rows):
        for box in range(2):
            source = box_anchor(meta_ref, source_row, box)
            skip = slot == box if source_row == target_row else None
            offsets = offsets_of(source, target, grid_tiles, skip)
            at = 2 * place + box
            copy = pltpu.make_async_copy(source_refs[place].at[box], stage.at[at], sems.at[at])
            pl.when(offsets[0])(copy.start)
            work.append((at, offsets, copy))
    for order_ref in (order_a, order_b):
        order_ref[0] = jnp.zeros((rows, LANES), jnp.float32)
        order_ref[chunks + 1] = jnp.zeros((rows, LANES), jnp.float32)
    total_copy.wait()
    part_copy.wait()
    if target_row == 2:
        total_ref[...] += part_stage[...]
    else:
        near_row = pl.multiple_of((1 - meta_ref[0, 8]) * half, half)
        total_ref[:, pl.ds(near_row, half), :] += part_stage[...]
    for at, offsets, copy in work:
        add_squares(total_ref, stage.at[at], offsets, ready=copy.wait)
    pltpu.make_async_copy(target_stage, target_stage, sems.at[2 * count]).wait()
    base = 1.0 + time_step * (growth_rate - 6.0 * gradient_energy)
    factor_ref = result_ref

    def prepare(at, carry):
        for group in range(groups):
            picked = pl.ds(group, groups, stride=groups)
            into = pl.ds(group * 8, 8)
            order_a[at + 1, into, :] = target_stage.at[at][picked, :]
            factor_ref[at, into, :] = (
                base - (time_step * 2.0 * coupling) * total_ref.at[at][picked, :]
            )
        return carry

    lax.fori_loop(0, chunks, prepare, 0, unroll=2)

    def deliver(at):
        columns = pl.ds(pl.multiple_of(at * LANES, LANES), LANES)
        pltpu.make_async_copy(
            total_ref.at[at], out_ref.at[out_slot, :, columns], sems.at[2 * count]
        ).start()

    relax_into((order_a, order_b), factor_ref, total_ref, rows, deliver)
    pltpu.make_async_copy(total_ref, total_ref, sems.at[2 * count]).wait()


def on_device(grain_boxes, box_anchors, migrations):
    _, box_edge, area = grain_boxes.shape
    devices = lax.axis_size("dev")
    position = lax.axis_index("dev")
    outward = (position % 2).astype(jnp.int32).reshape(1, 1)
    meta = jnp.concatenate([box_anchors.reshape(1, -1), migrations.reshape(1, -1)], axis=1)
    metas = [meta]
    for steps in (-1, 1, 2, 3):
        metas.append(from_outward(meta, steps))
    metas.append(from_outward(jnp.concatenate(metas[2:4], axis=0), -1))
    partner = from_outward(grain_boxes, -1)
    outer = from_outward(grain_boxes, 1)
    outer2 = from_outward(grain_boxes, 2)

    def with_flag(rows):
        rows = jnp.concatenate(rows, axis=0)
        return jnp.concatenate([rows, jnp.broadcast_to(outward, (rows.shape[0], 1))], axis=1)

    early_metas = with_flag(metas[:5])
    metas = with_flag(metas)

    smem = pl.BlockSpec(memory_space=pltpu.SMEM)
    vmem = pl.BlockSpec(memory_space=pltpu.VMEM)
    anywhere = pl.BlockSpec(memory_space=pl.ANY)
    chunks = area // LANES
    half_shape = jax.ShapeDtypeStruct((chunks, box_edge // 2, LANES), jnp.float32)
    box_shape = jax.ShapeDtypeStruct((chunks, box_edge, LANES), jnp.float32)
    full_part, near_part, outer_sum, inner_sum = pl.pallas_call(
        functools.partial(early_kernel, devices),
        out_shape=(box_shape, half_shape, box_shape, box_shape),
        in_specs=[smem, vmem, vmem],
        out_specs=(vmem,) * 4,
        name="early_sums",
        cost_estimate=pl.CostEstimate(flops=8_000_000, bytes_accessed=8_000_000, transcendentals=0),
    )(early_metas, grain_boxes, partner)
    full_sum = from_outward(full_part, 3)
    near_sum = from_outward(near_part, -4)
    inner2 = from_outward(outer, -1)
    inner3 = from_outward(outer2, -1)

    def relax(target_row, source_rows, total, part, target_boxes, sources, before):
        count = len(source_rows)
        aliased = 0 if before is None else 1
        box_scratch = pltpu.VMEM((chunks, box_edge, LANES), jnp.float32)
        padded = pltpu.VMEM((chunks + 2, box_edge, LANES), jnp.float32)
        extra = () if before is None else (before,)
        return pl.pallas_call(
            functools.partial(relax_kernel, devices, target_row, source_rows, aliased),
            out_shape=jax.ShapeDtypeStruct(grain_boxes.shape, jnp.float32),
            in_specs=[smem] + [anywhere] * (3 + count + aliased),
            out_specs=anywhere,
            input_output_aliases={4 + count: 0} if aliased else {},
            scratch_shapes=[
                padded,
                padded,
                box_scratch,
                box_scratch,
                pltpu.VMEM((2 * count, box_edge, area), jnp.float32),
                box_scratch,
                pltpu.VMEM(part.shape, jnp.float32),
                pltpu.SemaphoreType.DMA((2 * count + 3,)),
            ],
            name="relax_outer" if target_row == 2 else "relax_inner",
            compiler_params=pltpu.CompilerParams(vmem_limit_bytes=60 * 1024 * 1024),
            cost_estimate=pl.CostEstimate(
                flops=20_000_000, bytes_accessed=10_000_000, transcendentals=0
            ),
        )(metas, total, part, target_boxes, *sources, *extra)

    first = relax(2, (2, 5, 3), outer_sum, full_sum, outer, (outer, inner2, outer2), None)
    return relax(
        1, (2, 5, 3, 6), inner_sum, near_sum, partner, (outer, inner2, outer2, inner3), first
    )


def solution(mesh):
    in_specs = (P("dev", None, None), P("dev", None), P("dev", None))
    out_specs = P("dev", None, None)
    return jax.shard_map(
        on_device, mesh=mesh, in_specs=in_specs, out_specs=out_specs, check_vma=False
    )
```
